32 devices in a mesh: rad: 4 (over y, x), azi: 8 (over z, core).
Axes of the slice: x: 2, y: 2, z: 4, core: 2. Of those that a mesh axis runs over, the one named last changes fastest.
Arguments:
- density: float32 [32, 2048, 128], P('rad', 'azi'), may hold values from 0.1 to 2
- shift_cells: int32 [32], P('rad'), may hold values from 0 to 2047
- upwind_flags: int32 [32], P('rad'), may hold values 0 or 1
- courant: float32 [32, 128], P('rad'), may hold values from 0.05 to 0.9
- gain_factors: float32 [8, 128, 128], replicated, may hold values from -0.5 to 0.5
- rate_left: float32 [8, 128], replicated, may hold values from 0.1 to 1
- rate_right: float32 [8, 128], replicated, may hold values from -0.5 to 0.5
Outputs:
- evolved: float32 [32, 2048, 128], P('rad', 'azi')
The draws below stay inside these ranges and needn't reach their ends.
All inputs are finite; a program needn't handle non-finite values. No bound on the sum of `upwind_flags` on one device may be relied on, other than what follows from the above.
Results may differ from the reference program's by a relative error of at most 0.0001.
Values sent between devices are 32-bit elements; how exact they have to be, the bound alone decides.
A program may use at most 64 MiB of HBM per device.

```python
import math
import jax
import jax.numpy as jnp
from jax import lax

NB = 128
RANK = 8
NR = 32
NA = 2048


def touch_ends(array, rng, low, top_value):
    longest = array.shape.index(max(array.shape))
    spots = []
    for shift in (0, 1):
        where = [jax.random.randint(jax.random.fold_in(rng, axis), (), 0, length) for axis, length in enumerate(array.shape)]
        where[longest] = (where[longest] + shift) % array.shape[longest]
        spots.append(tuple(where))
    return array.at[spots[0]].set(low).at[spots[1]].set(top_value)


def shard_levels(stream_key, dims, split, low, high):
    level = 1.0
    for position, shards_of in split:
        heights = jax.random.uniform(jax.random.fold_in(jax.random.fold_in(stream_key, 6), position), (shards_of,), jnp.float32, low / len(split), high / len(split))
        level = level * jnp.repeat(jnp.exp(heights), dims[position] // shards_of).reshape((-1,) + (1,) * (len(dims) - 1 - position))
    return level


def normal_values(key, shape, scale, bound, dtype=jnp.bfloat16):
    array = scale * jax.random.normal(key, shape, jnp.float32)
    return jnp.clip(array, min=-bound, max=bound).astype(dtype)


def setup_inputs(seed: int = 0) -> dict:
    seeds = jax.random.split(jax.random.key(seed), 8)
    return {
        "density": jnp.clip(jnp.exp(math.log(2.0) - 2.9957323 * jax.random.uniform(seeds[0], (NR, NA, NB), jnp.float32) ** shard_levels(seeds[0], (NR, NA, NB), ((0, 4), (1, 8)), -0.2, 0.2)), 0.1, 2.0),
        "shift_cells": touch_ends(jax.random.randint(seeds[1], (NR,), 0, NA), jax.random.fold_in(seeds[1], 1), 0, NA - 1).astype(jnp.int32),
        "upwind_flags": touch_ends((jax.random.randint(seeds[2], (NR,), 0, 2) < 1).astype(jnp.int32), jax.random.fold_in(seeds[2], 1), 0, 1),
        "courant": jnp.clip(jnp.exp(math.log(0.9) - 2.8903717 * jax.random.uniform(seeds[3], (NR, NB), jnp.float32) ** shard_levels(seeds[3], (NR, NB), ((0, 4),), -0.2, 0.2)), 0.05, 0.9),
        "gain_factors": normal_values(seeds[4], (RANK, NB, NB), NB ** -0.5, 0.5, jnp.float32),
        "rate_left": jnp.clip(jnp.exp(jax.random.uniform(seeds[5], (RANK, NB), jnp.float32, math.log(0.1), math.log(1.0))), 0.1, 1.0),
        "rate_right": normal_values(seeds[6], (RANK, NB), NB ** -0.5, 0.5, jnp.float32),
    }


def roll_row(row, amount):
    return jnp.roll(row, amount, axis=0)


def coagulate(block, gain_factors, rate_left, rate_right):
    cells = block.reshape(-1, block.shape[-1])
    partner = jnp.dot(cells, rate_right.T, preferred_element_type=jnp.float32, precision=lax.Precision.HIGHEST)
    loss_rate = jnp.dot(partner, rate_left, preferred_element_type=jnp.float32, precision=lax.Precision.HIGHEST)
    gain = jnp.zeros_like(cells)
    for term in range(gain_factors.shape[0]):
        mapped = jnp.dot(cells, gain_factors[term], preferred_element_type=jnp.float32, precision=lax.Precision.HIGHEST)
        gain = gain + partner[:, term:term + 1] * mapped
    result = cells + 0.25 * (gain - cells * loss_rate)
    return result.reshape(block.shape)


def reference(density, shift_cells, upwind_flags, courant, gain_factors, rate_left, rate_right):
    shifted = jax.vmap(roll_row)(density, shift_cells)
    padded = jnp.pad(shifted, ((1, 1), (0, 0), (0, 0)))
    source = jnp.where((upwind_flags == 1)[:, None, None], padded[2:], padded[:-2])
    drifted = shifted - courant[:, None, :] * (shifted - source)
    return lax.map(lambda block: coagulate(block, gain_factors, rate_left, rate_right), drifted)
```

```python
import functools

import jax
import jax.numpy as jnp
from jax import lax
from jax.experimental import pallas as pl
from jax.experimental.pallas import tpu as pltpu
from jax.sharding import PartitionSpec as P

MESH = pl.DeviceIdType.MESH


def evolve(cells, left, split, rights):
    terms, bins = left.shape
    high = cells.astype(jnp.bfloat16)
    low = (cells - high.astype(jnp.float32)).astype(jnp.bfloat16)
    both = jnp.concatenate([high, low, high, low], axis=1)
    partner = lax.dot_general(
        both, rights[...], (((1,), (1,)), ((), ())), preferred_element_type=jnp.float32
    )
    change = jnp.zeros_like(cells)
    for p in range(0, terms, 2):
        pair = jnp.dot(both, split[:, p * bins : (p + 2) * bins], preferred_element_type=jnp.float32)
        for q in range(2):
            mapped = pair[:, q * bins : (q + 1) * bins] - cells * left[p + q : p + q + 1, :]
            change = change + partner[:, p + q : p + q + 1] * mapped
    return cells + 0.25 * change


def closing(tail, held, split, rights, left, out, last, sems):
    radii, length, bins = held.shape
    ready = pltpu.make_async_copy(held.at[pl.ds(0, radii - tail)], out.at[pl.ds(0, radii - tail)], sems.at[tail])
    ready.start()
    cells = held[radii - tail : radii].reshape(tail * length, bins)
    last[...] = evolve(cells, left, split, rights).reshape(tail, length, bins)
    sends = [pltpu.make_async_copy(last.at[i], out.at[radii - tail + i], sems.at[i]) for i in range(tail)]
    for send in sends:
        send.start()
    for send in sends:
        send.wait()
    ready.wait()


def kernel(
    n, bands, shift_in, flags_in, courant_in, left_in, right_in, density, factors, out, split, rights, left,
    shift, flags, courant, right,
    landing, work, send, recv, twice, ext, raw,
    s_first, r_first, s_second, r_second, s_halo, r_halo, s_small,
):
    radii, length, bins = density.shape
    rows = length // n
    terms = factors.shape[0]
    total = n * length
    me = lax.axis_index("azi")
    band = lax.axis_index("rad")
    outer = lax.rem(band + 1, bands)
    inner = lax.rem(band + bands - 1, bands)

    barrier = pltpu.get_barrier_semaphore()
    for d in range(1, n):
        pl.semaphore_signal(barrier, inc=1, device_id={"azi": lax.rem(me + d, n)}, device_id_type=MESH)
    for other in (outer, inner):
        pl.semaphore_signal(barrier, inc=1, device_id={"rad": other}, device_id_type=MESH)
    pl.semaphore_wait(barrier, n + 1)

    def radius_of(t):
        return lax.rem(t + radii - 1, radii)

    def first(t, _):
        pair = lax.rem(t + radii // 2 - 1, radii // 2)
        two = pl.ds(2 * pair, 2)
        for d in range(1, n):
            to = lax.rem(me + d, n)
            pltpu.make_async_remote_copy(
                src_ref=density.at[two, pl.ds(to * rows, rows)],
                dst_ref=landing.at[two, me],
                send_sem=s_first,
                recv_sem=r_first.at[pair],
                device_id={"azi": to},
                device_id_type=MESH,
            ).start()
        pltpu.make_async_copy(
            density.at[two, pl.ds(me * rows, rows)], landing.at[two, me], r_first.at[pair]
        ).start()
        return 0

    lax.fori_loop(0, radii // 2, first, 0)

    fetches = [
        pltpu.make_async_copy(a, b, s_small.at[i])
        for i, (a, b) in enumerate((
            (shift_in, shift), (flags_in, flags), (courant_in, courant), (left_in, left),
            (right_in, right), (factors, raw),
        ))
    ]
    for fetch in fetches:
        fetch.start()
    for fetch in fetches:
        fetch.wait()
    for p in range(terms):
        high = raw[p].astype(jnp.bfloat16)
        low = (raw[p] - high.astype(jnp.float32)).astype(jnp.bfloat16)
        columns = pl.ds(p * bins, bins)
        split[0:bins, columns] = high
        split[bins : 2 * bins, columns] = high
        split[2 * bins : 3 * bins, columns] = low
        split[3 * bins : 4 * bins, columns] = low

    high = right[...].astype(jnp.bfloat16)
    low = (right[...] - high.astype(jnp.float32)).astype(jnp.bfloat16)
    rights[...] = jnp.concatenate([high, high, low, low], axis=1)
    place = me * rows + lax.broadcasted_iota(jnp.int32, (rows, bins), 0)

    def landed(pair):
        two = landing.at[pl.ds(0, 2)]
        pltpu.make_async_copy(two, two, r_first.at[pair]).wait()

    landed(radii // 2 - 1)
    for pair in range(min(2, radii // 2 - 1)):
        landed(pair)

    def second(t, _):
        k = radius_of(t)
        @pl.when((lax.rem(t, 2) == 1) & (t < radii - 1 - 2 * 2))
        def _():
            landed(lax.div(t, 2) + 2)

        work[...] = landing[k]
        back = total - shift[k]
        keep = place >= lax.rem(back, length)
        block = lax.div(back, length)
        held = work[lax.rem(block, n)]
        for i in range(n):
            following = work[lax.rem(block + i + 1, n)]
            send[k, i] = jnp.where(keep, held, following)
            held = following
        recv[k, me] = send[k, me]
        for d in range(1, n):
            to = lax.rem(me + d, n)
            pltpu.make_async_remote_copy(
                src_ref=send.at[k, to],
                dst_ref=recv.at[k, me],
                send_sem=s_second,
                recv_sem=r_second.at[k],
                device_id={"azi": to},
                device_id_type=MESH,
            ).start()
        return 0

    lax.fori_loop(0, radii, second, 0)

    def arrive(t):
        k = radius_of(t)
        part = recv.at[k, pl.ds(0, n - 1)]
        pltpu.make_async_copy(part, part, r_second.at[k]).wait()
        return k

    def settle(k):
        whole = recv[k].reshape(length, bins)
        twice[0:length] = whole
        twice[length : 2 * length] = whole
        ext[k + 1] = twice[pl.ds(lax.rem(total - shift[k], length), length), :]

    def drift(k, below=None, above=None):
        here = ext[k + 1]
        low_side = ext[k]
        high_side = ext[k + 2]
        if below is not None:
            low_side = jnp.where(below, 0.0, low_side)
        if above is not None:
            high_side = jnp.where(above, 0.0, high_side)
        source = jnp.where(flags[k] == 1, high_side, low_side)
        return here - courant[pl.ds(k, 1), :] * (here - source)

    def coagulate(k, below=None, above=None):
        out[k] = evolve(drift(k, below, above), left, split, rights)

    settle(arrive(0))
    settle(arrive(1))
    following = arrive(2)
    to_outer = pltpu.make_async_remote_copy(
        src_ref=ext.at[radii], dst_ref=ext.at[0], send_sem=s_halo.at[0], recv_sem=r_halo.at[0],
        device_id={"rad": outer}, device_id_type=MESH,
    )
    to_inner = pltpu.make_async_remote_copy(
        src_ref=ext.at[1], dst_ref=ext.at[radii + 1], send_sem=s_halo.at[1], recv_sem=r_halo.at[1],
        device_id={"rad": inner}, device_id_type=MESH,
    )
    to_outer.start()
    to_inner.start()
    settle(following)

    def middle(t, _):
        settle(arrive(t))
        coagulate(t - 2)
        return 0

    lax.fori_loop(3, radii - 1, middle, 0)
    to_outer.wait()
    to_inner.wait()
    coagulate(0, below=band == 0)
    settle(arrive(radii - 1))
    out[radii - 3] = drift(radii - 3)
    out[radii - 2] = drift(radii - 2)
    out[radii - 1] = drift(radii - 1, above=band == bands - 1)
    sent = send.at[:, pl.ds(0, n - 1)]
    pltpu.make_async_copy(sent, sent, s_first).wait()
    pltpu.make_async_copy(sent, sent, s_second).wait()


def shards(n, bands, density, shift_cells, upwind_flags, courant, gain_factors, rate_left, rate_right):
    radii, length, bins = density.shape
    terms = gain_factors.shape[0]
    rows = length // n
    hbm = pl.BlockSpec(memory_space=pl.ANY)
    vmem = pl.BlockSpec(memory_space=pltpu.VMEM)
    real = jnp.float32
    room = 67043328 - 12 * radii * length * bins
    held, split, rights, left = pl.pallas_call(
        functools.partial(kernel, n, bands),
        out_shape=(
            pltpu.VMEM(density.shape, real),
            pltpu.VMEM((4 * bins, terms * bins), jnp.bfloat16),
            pltpu.VMEM((terms, 4 * bins), jnp.bfloat16),
            pltpu.VMEM((terms, bins), real),
        ),
        in_specs=[hbm] * 7,
        out_specs=(vmem,) * 4,
        scratch_shapes=[
            pltpu.SMEM((radii,), jnp.int32),
            pltpu.SMEM((radii,), jnp.int32),
            pltpu.VMEM((radii, bins), real),
            pltpu.VMEM((terms, bins), real),
            pltpu.VMEM((radii, n, rows, bins), real),
            pltpu.VMEM((n, rows, bins), real),
            pltpu.VMEM((radii, n, rows, bins), real),
            pltpu.VMEM((radii, n, rows, bins), real),
            pltpu.VMEM((2 * length, bins), real),
            pltpu.VMEM((radii + 2, length, bins), real),
            pltpu.VMEM((terms, bins, bins), real),
            pltpu.SemaphoreType.DMA,
            pltpu.SemaphoreType.DMA((radii,)),
            pltpu.SemaphoreType.DMA,
            pltpu.SemaphoreType.DMA((radii,)),
            pltpu.SemaphoreType.DMA((2,)),
            pltpu.SemaphoreType.DMA((2,)),
            pltpu.SemaphoreType.DMA((6,)),
        ],
        compiler_params=pltpu.CompilerParams(collective_id=0, has_side_effects=True, vmem_limit_bytes=room),
        name="advect_coagulate",
    )(shift_cells, upwind_flags, courant, rate_left, rate_right, density, gain_factors)
    tail = 3
    return pl.pallas_call(
        functools.partial(closing, tail),
        out_shape=jax.ShapeDtypeStruct(density.shape, real),
        in_specs=[vmem] * 4,
        out_specs=hbm,
        scratch_shapes=[pltpu.VMEM((tail, length, bins), real), pltpu.SemaphoreType.DMA((tail + 1,))],
        compiler_params=pltpu.CompilerParams(vmem_limit_bytes=room // 2),
        name="close",
    )(held, split, rights, left)


def solution(mesh):
    return jax.shard_map(
        functools.partial(shards, mesh.shape["azi"], mesh.shape["rad"]),
        mesh=mesh,
        in_specs=(P("rad", "azi", None), P("rad"), P("rad"), P("rad", None), P(), P(), P()),
        out_specs=P("rad", "azi", None),
        check_vma=False,
    )
```

```python
import functools

import jax
import jax.numpy as jnp
from jax import lax
from jax.experimental import pallas as pl
from jax.experimental.pallas import tpu as pltpu
from jax.sharding import PartitionSpec as P

MESH = pl.DeviceIdType.MESH


def evolve(cells, split, rights):
    bins = cells.shape[1]
    terms = split.shape[1] // bins
    high = cells.astype(jnp.bfloat16)
    low = (cells - high.astype(jnp.float32)).astype(jnp.bfloat16)
    both = jnp.concatenate([high, low, high], axis=1)
    rates = jnp.dot(both, rights[...], preferred_element_type=jnp.float32)
    partner = rates[:, bins : bins + terms]
    change = -cells * rates[:, :bins]
    for p in range(0, terms, 2):
        pair = jnp.dot(both, split[:, p * bins : (p + 2) * bins], preferred_element_type=jnp.float32)
        for q in range(2):
            change = change + partner[:, p + q : p + q + 1] * pair[:, q * bins : (q + 1) * bins]
    return cells + 0.25 * change


def closing(tail, held, split, rights, out, last, sems):
    radii, length, bins = held.shape
    ready = pltpu.make_async_copy(held.at[pl.ds(0, radii - tail)], out.at[pl.ds(0, radii - tail)], sems.at[tail])
    ready.start()
    cells = held[radii - tail : radii].reshape(tail * length, bins)
    last[...] = evolve(cells, split, rights).reshape(tail, length, bins)
    sends = [pltpu.make_async_copy(last.at[i], out.at[radii - tail + i], sems.at[i]) for i in range(tail)]
    for send in sends:
        send.start()
    for send in sends:
        send.wait()
    ready.wait()


def kernel(
    n, bands, shift_in, flags_in, courant_in, left_in, right_in, density, factors, out, split, rights,
    shift, flags, courant, left, right,
    landing, work, send, recv, twice, ext, raw,
    s_first, r_first, s_second, r_second, s_halo, r_halo, s_small,
):
    radii, length, bins = density.shape
    rows = length // n
    terms = factors.shape[0]
    total = n * length
    me = lax.axis_index("azi")
    band = lax.axis_index("rad")
    outer = lax.rem(band + 1, bands)
    inner = lax.rem(band + bands - 1, bands)

    barrier = pltpu.get_barrier_semaphore()
    for d in range(1, n):
        pl.semaphore_signal(barrier, inc=1, device_id={"azi": lax.rem(me + d, n)}, device_id_type=MESH)
    for other in (outer, inner):
        pl.semaphore_signal(barrier, inc=1, device_id={"rad": other}, device_id_type=MESH)
    pl.semaphore_wait(barrier, n + 1)

    def radius_of(t):
        return lax.rem(t + radii - 1, radii)

    def first(t, _):
        pair = lax.rem(t + radii // 2 - 1, radii // 2)
        two = pl.ds(2 * pair, 2)
        for d in range(1, n):
            to = lax.rem(me + d, n)
            pltpu.make_async_remote_copy(
                src_ref=density.at[two, pl.ds(to * rows, rows)],
                dst_ref=landing.at[two, me],
                send_sem=s_first,
                recv_sem=r_first.at[pair],
                device_id={"azi": to},
                device_id_type=MESH,
            ).start()
        pltpu.make_async_copy(
            density.at[two, pl.ds(me * rows, rows)], landing.at[two, me], r_first.at[pair]
        ).start()
        return 0

    lax.fori_loop(0, radii // 2, first, 0)

    fetches = [
        pltpu.make_async_copy(a, b, s_small.at[i])
        for i, (a, b) in enumerate((
            (shift_in, shift), (flags_in, flags), (courant_in, courant), (left_in, left),
            (right_in, right), (factors, raw),
        ))
    ]
    for fetch in fetches:
        fetch.start()
    for fetch in fetches:
        fetch.wait()
    for p in range(terms):
        high = raw[p].astype(jnp.bfloat16)
        low = (raw[p] - high.astype(jnp.float32)).astype(jnp.bfloat16)
        columns = pl.ds(p * bins, bins)
        split[0:bins, columns] = high
        split[bins : 2 * bins, columns] = high
        split[2 * bins : 3 * bins, columns] = low

    loss = lax.dot_general(
        right[...], left[...], (((0,), (0,)), ((), ())),
        precision=lax.Precision.HIGHEST, preferred_element_type=jnp.float32,
    )
    turned = jnp.concatenate([right[...], jnp.zeros((bins - terms, bins), jnp.float32)], axis=0).T
    exact = jnp.concatenate([loss, turned], axis=1)
    high = exact.astype(jnp.bfloat16)
    low = (exact - high.astype(jnp.float32)).astype(jnp.bfloat16)
    rights[...] = jnp.concatenate([high, high, low], axis=0)
    place = me * rows + lax.broadcasted_iota(jnp.int32, (rows, bins), 0)

    def landed(pair):
        two = landing.at[pl.ds(0, 2)]
        pltpu.make_async_copy(two, two, r_first.at[pair]).wait()

    landed(radii // 2 - 1)
    for pair in range(min(2, radii // 2 - 1)):
        landed(pair)

    def second(t, _):
        k = radius_of(t)
        @pl.when((lax.rem(t, 2) == 1) & (t < radii - 1 - 2 * 2))
        def _():
            landed(lax.div(t, 2) + 2)

        work[...] = landing[k]
        back = total - shift[k]
        keep = place >= lax.rem(back, length)
        block = lax.div(back, length)
        held = work[lax.rem(block, n)]
        for i in range(n):
            following = work[lax.rem(block + i + 1, n)]
            send[k, i] = jnp.where(keep, held, following)
            held = following
        recv[k, me] = send[k, me]
        for d in range(1, n):
            to = lax.rem(me + d, n)
            pltpu.make_async_remote_copy(
                src_ref=send.at[k, to],
                dst_ref=recv.at[k, me],
                send_sem=s_second,
                recv_sem=r_second.at[k],
                device_id={"azi": to},
                device_id_type=MESH,
            ).start()
        return 0

    lax.fori_loop(0, radii, second, 0)

    def arrive(t):
        k = radius_of(t)
        part = recv.at[k, pl.ds(0, n - 1)]
        pltpu.make_async_copy(part, part, r_second.at[k]).wait()
        return k

    def settle(k):
        whole = recv[k].reshape(length, bins)
        twice[0:length] = whole
        twice[length : 2 * length] = whole
        ext[k + 1] = twice[pl.ds(lax.rem(total - shift[k], length), length), :]

    def drift(k, below=None, above=None):
        here = ext[k + 1]
        low_side = ext[k]
        high_side = ext[k + 2]
        if below is not None:
            low_side = jnp.where(below, 0.0, low_side)
        if above is not None:
            high_side = jnp.where(above, 0.0, high_side)
        source = jnp.where(flags[k] == 1, high_side, low_side)
        return here - courant[pl.ds(k, 1), :] * (here - source)

    def coagulate(k, below=None, above=None):
        out[k] = evolve(drift(k, below, above), split, rights)

    settle(arrive(0))
    settle(arrive(1))
    following = arrive(2)
    to_outer = pltpu.make_async_remote_copy(
        src_ref=ext.at[radii], dst_ref=ext.at[0], send_sem=s_halo.at[0], recv_sem=r_halo.at[0],
        device_id={"rad": outer}, device_id_type=MESH,
    )
    to_inner = pltpu.make_async_remote_copy(
        src_ref=ext.at[1], dst_ref=ext.at[radii + 1], send_sem=s_halo.at[1], recv_sem=r_halo.at[1],
        device_id={"rad": inner}, device_id_type=MESH,
    )
    to_outer.start()
    to_inner.start()
    settle(following)

    def middle(t, _):
        settle(arrive(t))
        coagulate(t - 2)
        return 0

    lax.fori_loop(3, radii - 1, middle, 0)
    to_outer.wait()
    to_inner.wait()
    coagulate(0, below=band == 0)
    settle(arrive(radii - 1))
    out[radii - 3] = drift(radii - 3)
    out[radii - 2] = drift(radii - 2)
    out[radii - 1] = drift(radii - 1, above=band == bands - 1)
    sent = send.at[:, pl.ds(0, n - 1)]
    pltpu.make_async_copy(sent, sent, s_first).wait()
    pltpu.make_async_copy(sent, sent, s_second).wait()


def shards(n, bands, density, shift_cells, upwind_flags, courant, gain_factors, rate_left, rate_right):
    radii, length, bins = density.shape
    terms = gain_factors.shape[0]
    rows = length // n
    hbm = pl.BlockSpec(memory_space=pl.ANY)
    vmem = pl.BlockSpec(memory_space=pltpu.VMEM)
    real = jnp.float32
    room = 67043328 - 12 * radii * length * bins
    held, split, rights = pl.pallas_call(
        functools.partial(kernel, n, bands),
        out_shape=(
            pltpu.VMEM(density.shape, real),
            pltpu.VMEM((3 * bins, terms * bins), jnp.bfloat16),
            pltpu.VMEM((3 * bins, 2 * bins), jnp.bfloat16),
        ),
        in_specs=[hbm] * 7,
        out_specs=(vmem,) * 3,
        scratch_shapes=[
            pltpu.SMEM((radii,), jnp.int32),
            pltpu.SMEM((radii,), jnp.int32),
            pltpu.VMEM((radii, bins), real),
            pltpu.VMEM((terms, bins), real),
            pltpu.VMEM((terms, bins), real),
            pltpu.VMEM((radii, n, rows, bins), real),
            pltpu.VMEM((n, rows, bins), real),
            pltpu.VMEM((radii, n, rows, bins), real),
            pltpu.VMEM((radii, n, rows, bins), real),
            pltpu.VMEM((2 * length, bins), real),
            pltpu.VMEM((radii + 2, length, bins), real),
            pltpu.VMEM((terms, bins, bins), real),
            pltpu.SemaphoreType.DMA,
            pltpu.SemaphoreType.DMA((radii,)),
            pltpu.SemaphoreType.DMA,
            pltpu.SemaphoreType.DMA((radii,)),
            pltpu.SemaphoreType.DMA((2,)),
            pltpu.SemaphoreType.DMA((2,)),
            pltpu.SemaphoreType.DMA((6,)),
        ],
        compiler_params=pltpu.CompilerParams(collective_id=0, has_side_effects=True, vmem_limit_bytes=room),
        name="advect_coagulate",
    )(shift_cells, upwind_flags, courant, rate_left, rate_right, density, gain_factors)
    tail = 3
    return pl.pallas_call(
        functools.partial(closing, tail),
        out_shape=jax.ShapeDtypeStruct(density.shape, real),
        in_specs=[vmem] * 3,
        out_specs=hbm,
        scratch_shapes=[pltpu.VMEM((tail, length, bins), real), pltpu.SemaphoreType.DMA((tail + 1,))],
        compiler_params=pltpu.CompilerParams(vmem_limit_bytes=room // 2),
        name="close",
    )(held, split, rights)


def solution(mesh):
    return jax.shard_map(
        functools.partial(shards, mesh.shape["azi"], mesh.shape["rad"]),
        mesh=mesh,
        in_specs=(P("rad", "azi", None), P("rad"), P("rad"), P("rad", None), P(), P(), P()),
        out_specs=P("rad", "azi", None),
        check_vma=False,
    )
```

```python
import functools

import jax
import jax.numpy as jnp
from jax import lax
from jax.experimental import pallas as pl
from jax.experimental.pallas import tpu as pltpu
from jax.sharding import PartitionSpec as P

MESH = pl.DeviceIdType.MESH


def evolve(cells, left, split, rights):
    terms, bins = left.shape
    high = cells.astype(jnp.bfloat16)
    low = (cells - high.astype(jnp.float32)).astype(jnp.bfloat16)
    both = jnp.concatenate([high, low, high, low], axis=1)
    partner = lax.dot_general(
        both, rights[...], (((1,), (1,)), ((), ())), preferred_element_type=jnp.float32
    )
    change = jnp.zeros_like(cells)
    for p in range(0, terms, 2):
        pair = jnp.dot(both, split[:, p * bins : (p + 2) * bins], preferred_element_type=jnp.float32)
        for q in range(2):
            mapped = pair[:, q * bins : (q + 1) * bins] - cells * left[p + q : p + q + 1, :]
            change = change + partner[:, p + q : p + q + 1] * mapped
    return cells + 0.25 * change


def closing(tail, held, split, rights, left, out, last, sems):
    radii, length, bins = held.shape
    ready = pltpu.make_async_copy(held.at[pl.ds(0, radii - tail)], out.at[pl.ds(0, radii - tail)], sems.at[tail])
    ready.start()
    cells = held[radii - tail : radii].reshape(tail * length, bins)
    last[...] = evolve(cells, left, split, rights).reshape(tail, length, bins)
    sends = [pltpu.make_async_copy(last.at[i], out.at[radii - tail + i], sems.at[i]) for i in range(tail)]
    for send in sends:
        send.start()
    for send in sends:
        send.wait()
    ready.wait()


def kernel(
    n, bands, shift_in, flags_in, courant_in, left_in, right_in, density, factors, out, split, rights, left,
    shift, flags, courant, right,
    landing, work, send, recv, twice, ext, raw,
    s_first, r_first, s_second, r_second, s_halo, r_halo, s_small,
):
    radii, length, bins = density.shape
    rows = length // n
    terms = factors.shape[0]
    total = n * length
    me = lax.axis_index("azi")
    band = lax.axis_index("rad")
    outer = lax.rem(band + 1, bands)
    inner = lax.rem(band + bands - 1, bands)

    barrier = pltpu.get_barrier_semaphore()
    for d in range(1, n):
        pl.semaphore_signal(barrier, inc=1, device_id={"azi": lax.rem(me + d, n)}, device_id_type=MESH)
    for other in (outer, inner):
        pl.semaphore_signal(barrier, inc=1, device_id={"rad": other}, device_id_type=MESH)
    pl.semaphore_wait(barrier, n + 1)

    def radius_of(t):
        return lax.rem(t + radii - 1, radii)

    def first(t, _):
        pair = lax.rem(t + radii // 2 - 1, radii // 2)
        two = pl.ds(2 * pair, 2)
        for d in range(1, n):
            to = lax.rem(me + d, n)
            pltpu.make_async_remote_copy(
                src_ref=density.at[two, pl.ds(to * rows, rows)],
                dst_ref=landing.at[two, me],
                send_sem=s_first,
                recv_sem=r_first.at[pair],
                device_id={"azi": to},
                device_id_type=MESH,
            ).start()
        pltpu.make_async_copy(
            density.at[two, pl.ds(me * rows, rows)], landing.at[two, me], r_first.at[pair]
        ).start()
        return 0

    lax.fori_loop(0, radii // 2, first, 0)

    fetches = [
        pltpu.make_async_copy(a, b, s_small.at[i])
        for i, (a, b) in enumerate((
            (shift_in, shift), (flags_in, flags), (courant_in, courant), (left_in, left),
            (right_in, right), (factors, raw),
        ))
    ]
    for fetch in fetches:
        fetch.start()
    for fetch in fetches:
        fetch.wait()
    for p in range(terms):
        high = raw[p].astype(jnp.bfloat16)
        low = (raw[p] - high.astype(jnp.float32)).astype(jnp.bfloat16)
        columns = pl.ds(p * bins, bins)
        split[0:bins, columns] = high
        split[bins : 2 * bins, columns] = high
        split[2 * bins : 3 * bins, columns] = low
        split[3 * bins : 4 * bins, columns] = low

    high = right[...].astype(jnp.bfloat16)
    low = (right[...] - high.astype(jnp.float32)).astype(jnp.bfloat16)
    rights[...] = jnp.concatenate([high, high, low, low], axis=1)
    place = me * rows + lax.broadcasted_iota(jnp.int32, (rows, bins), 0)

    def landed(pair):
        two = landing.at[pl.ds(0, 2)]
        pltpu.make_async_copy(two, two, r_first.at[pair]).wait()

    landed(radii // 2 - 1)
    for pair in range(min(2, radii // 2 - 1)):
        landed(pair)

    def second(t, _):
        k = radius_of(t)
        @pl.when((lax.rem(t, 2) == 1) & (t < radii - 1 - 2 * 2))
        def _():
            landed(lax.div(t, 2) + 2)

        work[...] = landing[k]
        back = total - shift[k]
        keep = place >= lax.rem(back, length)
        block = lax.div(back, length)
        held = work[lax.rem(block, n)]
        for i in range(n):
            following = work[lax.rem(block + i + 1, n)]
            send[k, i] = jnp.where(keep, held, following)
            held = following
        recv[k, me] = send[k, me]
        for d in sorted(range(1, n), key=lambda d: abs(d - n // 2)):
            to = lax.rem(me + d, n)
            pltpu.make_async_remote_copy(
                src_ref=send.at[k, to],
                dst_ref=recv.at[k, me],
                send_sem=s_second,
                recv_sem=r_second.at[k],
                device_id={"azi": to},
                device_id_type=MESH,
            ).start()
        return 0

    lax.fori_loop(0, radii, second, 0)

    def arrive(t):
        k = radius_of(t)
        part = recv.at[k, pl.ds(0, n - 1)]
        pltpu.make_async_copy(part, part, r_second.at[k]).wait()
        return k

    def settle(k):
        whole = recv[k].reshape(length, bins)
        twice[0:length] = whole
        twice[length : 2 * length] = whole
        ext[k + 1] = twice[pl.ds(lax.rem(total - shift[k], length), length), :]

    def drift(k, below=None, above=None):
        here = ext[k + 1]
        low_side = ext[k]
        high_side = ext[k + 2]
        if below is not None:
            low_side = jnp.where(below, 0.0, low_side)
        if above is not None:
            high_side = jnp.where(above, 0.0, high_side)
        source = jnp.where(flags[k] == 1, high_side, low_side)
        return here - courant[pl.ds(k, 1), :] * (here - source)

    def coagulate(k, below=None, above=None):
        out[k] = evolve(drift(k, below, above), left, split, rights)

    settle(arrive(0))
    settle(arrive(1))
    following = arrive(2)
    to_outer = pltpu.make_async_remote_copy(
        src_ref=ext.at[radii], dst_ref=ext.at[0], send_sem=s_halo.at[0], recv_sem=r_halo.at[0],
        device_id={"rad": outer}, device_id_type=MESH,
    )
    to_inner = pltpu.make_async_remote_copy(
        src_ref=ext.at[1], dst_ref=ext.at[radii + 1], send_sem=s_halo.at[1], recv_sem=r_halo.at[1],
        device_id={"rad": inner}, device_id_type=MESH,
    )
    to_outer.start()
    to_inner.start()
    settle(following)

    def middle(t, _):
        settle(arrive(t))
        coagulate(t - 2)
        return 0

    lax.fori_loop(3, radii - 1, middle, 0)
    to_outer.wait()
    to_inner.wait()
    coagulate(0, below=band == 0)
    settle(arrive(radii - 1))
    out[radii - 3] = drift(radii - 3)
    out[radii - 2] = drift(radii - 2)
    out[radii - 1] = drift(radii - 1, above=band == bands - 1)
    sent = send.at[:, pl.ds(0, n - 1)]
    pltpu.make_async_copy(sent, sent, s_first).wait()
    pltpu.make_async_copy(sent, sent, s_second).wait()


def shards(n, bands, density, shift_cells, upwind_flags, courant, gain_factors, rate_left, rate_right):
    radii, length, bins = density.shape
    terms = gain_factors.shape[0]
    rows = length // n
    hbm = pl.BlockSpec(memory_space=pl.ANY)
    vmem = pl.BlockSpec(memory_space=pltpu.VMEM)
    real = jnp.float32
    room = 67043328 - 12 * radii * length * bins
    held, split, rights, left = pl.pallas_call(
        functools.partial(kernel, n, bands),
        out_shape=(
            pltpu.VMEM(density.shape, real),
            pltpu.VMEM((4 * bins, terms * bins), jnp.bfloat16),
            pltpu.VMEM((terms, 4 * bins), jnp.bfloat16),
            pltpu.VMEM((terms, bins), real),
        ),
        in_specs=[hbm] * 7,
        out_specs=(vmem,) * 4,
        scratch_shapes=[
            pltpu.SMEM((radii,), jnp.int32),
            pltpu.SMEM((radii,), jnp.int32),
            pltpu.VMEM((radii, bins), real),
            pltpu.VMEM((terms, bins), real),
            pltpu.VMEM((radii, n, rows, bins), real),
            pltpu.VMEM((n, rows, bins), real),
            pltpu.VMEM((radii, n, rows, bins), real),
            pltpu.VMEM((radii, n, rows, bins), real),
            pltpu.VMEM((2 * length, bins), real),
            pltpu.VMEM((radii + 2, length, bins), real),
            pltpu.VMEM((terms, bins, bins), real),
            pltpu.SemaphoreType.DMA,
            pltpu.SemaphoreType.DMA((radii,)),
            pltpu.SemaphoreType.DMA,
            pltpu.SemaphoreType.DMA((radii,)),
            pltpu.SemaphoreType.DMA((2,)),
            pltpu.SemaphoreType.DMA((2,)),
            pltpu.SemaphoreType.DMA((6,)),
        ],
        compiler_params=pltpu.CompilerParams(collective_id=0, has_side_effects=True, vmem_limit_bytes=room),
        name="advect_coagulate",
    )(shift_cells, upwind_flags, courant, rate_left, rate_right, density, gain_factors)
    tail = 3
    return pl.pallas_call(
        functools.partial(closing, tail),
        out_shape=jax.ShapeDtypeStruct(density.shape, real),
        in_specs=[vmem] * 4,
        out_specs=hbm,
        scratch_shapes=[pltpu.VMEM((tail, length, bins), real), pltpu.SemaphoreType.DMA((tail + 1,))],
        compiler_params=pltpu.CompilerParams(vmem_limit_bytes=room // 2),
        name="close",
    )(held, split, rights, left)


def solution(mesh):
    return jax.shard_map(
        functools.partial(shards, mesh.shape["azi"], mesh.shape["rad"]),
        mesh=mesh,
        in_specs=(P("rad", "azi", None), P("rad"), P("rad"), P("rad", None), P(), P(), P()),
        out_specs=P("rad", "azi", None),
        check_vma=False,
    )
```
